32 devices in a mesh: section: 2 (over y), tensor: 4 (over x, core), dp: 4 (over z).
Axes of the slice: x: 2, y: 2, z: 4, core: 2. Of those that a mesh axis runs over, the one named last changes fastest.
Arguments:
- hidden: bfloat16 [2, 8, 256, 14336], P('section', 'dp', None, 'tensor'), parts along dimension 1, may hold values from -6 to 6
- down_weight: bfloat16 [2, 14336, 4096], P('section', 'tensor'), may hold values from -0.046875 to 0.046875
- residual: bfloat16 [2, 8, 256, 4096], P('section', 'dp', 'tensor'), parts along dimension 1, may hold values from -6 to 6
- norm_gain: float32 [2, 4096], P('section'), may hold values from 0.1 to 1.9
- qkv_weight: bfloat16 [2, 4096, 5120], P('section', None, 'tensor'), may hold values from -0.09375 to 0.09375
Outputs:
- carried: bfloat16 [2, 8, 256, 4096], P('section', 'dp', 'tensor'), parts along dimension 1
- attention_inputs: bfloat16 [2, 8, 256, 5120], P('section', 'dp', None, 'tensor'), parts along dimension 1
The draws below stay inside these ranges and needn't reach their ends.
There are 4 independent parts, one for each index of `dp`. The reference program is written for one: setup_inputs(seed, part) draws one part's arguments, and reference() takes and returns one part's arrays. A program takes and returns all parts, laid end to end along the dimension named above; an argument that names none is the same for every part. Nothing has to cross between parts.
All inputs are finite; a program needn't handle non-finite values.
Results may differ from the reference program's by a relative error of at most 0.012.
Values may be sent and summed in bfloat16 or wider, within the bound.
A program may use at most 128 MiB of HBM per device.

```python
import jax
import jax.numpy as jnp
from jax import lax

D = 4096
FF = 14336
QKV = 5120
MB = 2
TOK = 256
SECTIONS = 2
N_TENSOR = 4


def level_of(own_key, extent, pieces, smallest, largest):
    loudness, own = 1.0, jax.random.fold_in(own_key, 6)
    for position, parts in pieces:
        heights = jnp.exp(jax.random.uniform(jax.random.fold_in(own, position), (parts,), jnp.float32, smallest / len(pieces), largest / len(pieces)))
        loudness = loudness * jnp.repeat(heights, extent[position] // parts).reshape([-1 if axis == position else 1 for axis in range(len(extent))])
    return loudness


def scatter_about(key, shape, deviation, reach, cuts=(), held_as=jnp.bfloat16):
    values = deviation * jax.random.normal(key, shape, jnp.float32)
    if cuts:
        values = values * level_of(key, shape, cuts, -0.22, 0.18)
    return jnp.clip(values, -reach, reach).astype(held_as)


def setup_inputs(seed: int = 0, part: int = 0) -> dict:
    splits = jax.random.split(jax.random.key(seed), 6)
    part_splits = jax.random.split(jax.random.fold_in(splits[5], part), 6)
    hidden = scatter_about(part_splits[0], (SECTIONS, MB, TOK, FF), 1.0, 6.0, ((0, 2), (3, 4)))
    down_weight = scatter_about(splits[1], (SECTIONS, FF, D), FF ** -0.5, 0.046875, ((0, 2), (1, 4)))
    residual = scatter_about(part_splits[2], (SECTIONS, MB, TOK, D), 1.0, 6.0, ((0, 2), (2, 4)))
    norm_gain = jnp.clip(1.0 + 0.18 * jax.random.normal(splits[3], (SECTIONS, D), jnp.float32), 0.1, 1.9)
    qkv_weight = scatter_about(splits[4], (SECTIONS, D, QKV), D ** -0.5, 0.09375, ((0, 2), (2, 4)))
    return {"hidden": hidden, "down_weight": down_weight, "residual": residual, "norm_gain": norm_gain, "qkv_weight": qkv_weight}


def section_stream(hidden_s, weight_s, residual_s):
    block = FF // N_TENSOR
    rows = hidden_s.reshape(MB * TOK, FF)

    def add_block(total, block_index):
        first = (block_index * block).astype(jnp.int32)
        hidden_part = lax.dynamic_slice_in_dim(rows, first, block, 1)
        weight_part = lax.dynamic_slice_in_dim(weight_s, first, block, 0)
        partial_value = jnp.dot(hidden_part, weight_part, preferred_element_type=jnp.float32).astype(jnp.bfloat16)
        partial_value = lax.optimization_barrier(partial_value)
        return (total + partial_value.astype(jnp.float32), None)
    start_total = jnp.zeros((MB * TOK, D), jnp.float32)
    total, _ = lax.scan(add_block, start_total, jnp.arange(N_TENSOR, dtype=jnp.int32))
    summed = total.reshape(MB, TOK, D) + residual_s.astype(jnp.float32)
    return summed.astype(jnp.bfloat16)

def reference(hidden, down_weight, residual, norm_gain, qkv_weight):
    streams = jnp.stack([section_stream(hidden[s], down_weight[s], residual[s]) for s in range(SECTIONS)])
    carried = jnp.roll(streams, 1, axis=0)
    outputs = []
    for s in range(SECTIONS):
        values = carried[s].astype(jnp.float32)
        mean_square = lax.optimization_barrier(jnp.mean(values * values, axis=-1, keepdims=True))
        normed = (values * lax.rsqrt(mean_square + 1e-05) * norm_gain[s][None, None, :]).astype(jnp.bfloat16)
        projected = jnp.dot(normed.reshape(MB * TOK, D), qkv_weight[s], preferred_element_type=jnp.float32)
        outputs.append(projected.astype(jnp.bfloat16).reshape(MB, TOK, QKV))
    return (carried, jnp.stack(outputs))
```

```python
import functools

import jax
import jax.numpy as jnp
from jax import lax
from jax.experimental import pallas as pl
from jax.experimental.pallas import tpu as pltpu
from jax.sharding import PartitionSpec as P

MESH = pl.DeviceIdType.MESH
F32 = jnp.float32
BF16 = jnp.bfloat16
CHUNKS = 8
SLABS = 3
LAG_X, LAG_SUM, LAG_HAND, LAG_PASS, LAG_PROJ = 1, 3, 5, 6, 7


def kernel(
    sections, tensor, hidden, weight, residual, gain, projector,
    carried_out, projected_out,
    rows, slab, qkv, res, own, core_send, core_recv, x_send, x_recv, base, stream, carried, acc, squares, out,
    hidden_sem, slab_sem, qkv_sem, res_sem, carried_sem, out_sem,
    core_ss, core_rs, x_ss, x_rs, y_ss, y_rs, g_ss, g_rs, c_ss, c_rs,
):
    chips = tensor // 2
    chunks, micro, local, width = stream.shape
    features = chunks * width
    depth = rows.shape[-1]
    half = chips * micro * local
    total = 2 * half
    s = lax.axis_index("section")
    t = lax.axis_index("tensor")
    chip, core = t // 2, lax.rem(t, 2)
    sibling = chip * 2 + 1 - core
    following = lax.rem(s + 1, sections)
    previous = lax.rem(s + sections - 1, sections)

    def ahead(j):
        return lax.rem(chip + j, chips)

    def behind(j):
        return lax.rem(chip + chips - j, chips)

    def hidden_copy(side, c, m):
        lane = 1 - core if side == 0 else core
        first = pl.multiple_of((c * 2 + lane) * local, local)
        return pltpu.make_async_copy(
            hidden.at[0, m, pl.ds(first, local), :], rows.at[side, c, m], hidden_sem.at[side, c, m]
        )

    def columns(k):
        return pl.ds(pl.multiple_of(k * width, width), width)

    def slab_copy(k):
        slot = lax.rem(k, SLABS)
        return pltpu.make_async_copy(weight.at[0, :, columns(k)], slab.at[slot], slab_sem.at[slot])

    def qkv_copy(k):
        return pltpu.make_async_copy(projector.at[0, columns(k), :], qkv.at[k], qkv_sem.at[k])

    res_copy = pltpu.make_async_copy(residual.at[0], res, res_sem)

    def carried_copy(k):
        return pltpu.make_async_copy(carried.at[k, t], carried_out.at[0, :, :, columns(k)], carried_sem.at[k])

    def out_copy(b, m):
        return pltpu.make_async_copy(
            out.at[b, m], projected_out.at[0, m, pl.ds(b * local, local), :], out_sem.at[b, m]
        )

    def core_copy(k):
        return pltpu.make_async_remote_copy(
            src_ref=core_send.at[k], dst_ref=core_recv.at[k], send_sem=core_ss.at[k], recv_sem=core_rs.at[k],
            device_id={"tensor": sibling}, device_id_type=MESH,
        )

    def x_copy(k, j):
        return pltpu.make_async_remote_copy(
            src_ref=x_send.at[k, j - 1], dst_ref=x_recv.at[k, j - 1],
            send_sem=x_ss.at[k, j - 1], recv_sem=x_rs.at[k, j - 1],
            device_id={"tensor": ahead(j) * 2 + core}, device_id_type=MESH,
        )

    def y_copy(k):
        return pltpu.make_async_remote_copy(
            src_ref=stream.at[k], dst_ref=carried.at[k, t], send_sem=y_ss.at[k], recv_sem=y_rs.at[k],
            device_id={"section": following}, device_id_type=MESH,
        )

    def gather_copy(k, j, block):
        return pltpu.make_async_remote_copy(
            src_ref=carried.at[k, block], dst_ref=carried.at[k, block],
            send_sem=g_ss.at[k, j - 1], recv_sem=g_rs.at[k, j - 1],
            device_id={"tensor": ahead(j) * 2 + core}, device_id_type=MESH,
        )

    def pass_copy(k, j, block):
        return pltpu.make_async_remote_copy(
            src_ref=carried.at[k, block], dst_ref=carried.at[k, block],
            send_sem=c_ss.at[k, j], recv_sem=c_rs.at[k, j],
            device_id={"tensor": sibling}, device_id_type=MESH,
        )

    for side in range(2):
        for c in range(chips):
            for m in range(micro):
                hidden_copy(side, c, m).start()
        if side == 0:
            slab_copy(0).start()
    res_copy.start()
    for k in range(1, SLABS):
        slab_copy(k).start()

    barrier = pltpu.get_barrier_semaphore()
    pl.semaphore_signal(barrier, inc=1, device_id={"tensor": sibling}, device_id_type=MESH)
    for j in range(1, chips):
        pl.semaphore_signal(barrier, inc=1, device_id={"tensor": ahead(j) * 2 + core}, device_id_type=MESH)
    pl.semaphore_signal(barrier, inc=1, device_id={"section": following}, device_id_type=MESH)
    if sections > 2:
        pl.semaphore_signal(barrier, inc=1, device_id={"section": previous}, device_id_type=MESH)
    pl.semaphore_wait(barrier, chips + (2 if sections > 2 else 1))

    acc[...] = jnp.zeros_like(acc)
    squares[...] = jnp.zeros_like(squares)

    def multiply(side, slot):
        product = jnp.dot(rows[side].reshape(half, depth), slab[slot], preferred_element_type=F32)
        return product.reshape(chips, micro, local, width)

    def step(i, _):
        @pl.when(i < chunks)
        def _():
            slot = lax.rem(i, SLABS)

            @pl.when(i == 0)
            def _():
                for c in range(chips):
                    for m in range(micro):
                        hidden_copy(0, c, m).wait()

            slab_copy(i).wait()
            core_send[i] = multiply(0, slot).astype(BF16)
            core_copy(i).start()

            @pl.when(i == 0)
            def _():
                for c in range(chips):
                    for m in range(micro):
                        hidden_copy(1, c, m).wait()
                res_copy.wait()

            own[lax.rem(i, 2)] = multiply(1, slot)

            @pl.when(i + SLABS < chunks)
            def _():
                slab_copy(i + SLABS).start()

            qkv_copy(i).start()

        k_x = i - LAG_X

        @pl.when((k_x >= 0) & (k_x < chunks))
        def _():
            k = k_x
            slot = lax.rem(k, 2)
            core_copy(k).wait_recv()
            for j in range(1, chips):
                x_send[k, j - 1] = (own[slot, ahead(j)] + core_recv[k, ahead(j)].astype(F32)).astype(BF16)
                x_copy(k, j).start()
            base[k] = own[slot, chip] + core_recv[k, chip].astype(F32) + res[:, :, columns(k)].astype(F32)

        k_sum = i - LAG_SUM

        @pl.when((k_sum >= 0) & (k_sum < chunks))
        def _():
            k = k_sum
            value = base[k]
            for j in range(1, chips):
                x_copy(k, j).wait_recv()
                value = value + x_recv[k, j - 1].astype(F32)
            stream[k] = value.astype(BF16)
            y_copy(k).start()

        k_hand = i - LAG_HAND

        @pl.when((k_hand >= 0) & (k_hand < chunks))
        def _():
            k = k_hand
            y_copy(k).wait_recv()
            for j in range(1, chips):
                gather_copy(k, j, t).start()
            pass_copy(k, 0, t).start()
            carried_copy(k).start()

        k_pass = i - LAG_PASS

        @pl.when((k_pass >= 0) & (k_pass < chunks))
        def _():
            k = k_pass
            for j in range(1, chips):
                block = behind(j) * 2 + core
                gather_copy(k, j, block).wait_recv()
                pass_copy(k, j, block).start()

        k_proj = i - LAG_PROJ

        @pl.when((k_proj >= 0) & (k_proj < chunks))
        def _():
            k = k_proj
            qkv_copy(k).wait()
            for j in range(chips):
                pass_copy(k, j, behind(j) * 2 + 1 - core).wait_recv()
            values = carried[k].reshape(total, width).astype(F32)
            squared = values * values
            part = squared[:, :128]
            for lane in range(128, width, 128):
                part = part + squared[:, lane:lane + 128]
            squares[...] += part
            scaled = (values * gain[:, columns(k)]).astype(BF16)
            acc[...] += jnp.dot(scaled, qkv[k], preferred_element_type=F32)

        return 0

    lax.fori_loop(0, chunks + LAG_PROJ, step, 0)

    block_rows = micro * local
    for b in range(tensor):
        lines = pl.ds(b * block_rows, block_rows)
        mean = jnp.sum(squares[lines, :], axis=-1, keepdims=True) * (1.0 / features)
        value = acc[lines, :] * lax.rsqrt(mean + 1e-05)
        out[b] = value.astype(BF16).reshape(out.shape[1:])
        for m in range(micro):
            out_copy(b, m).start()

    def drain(k, _):
        core_copy(k).wait_send()
        y_copy(k).wait_send()
        carried_copy(k).wait()
        pass_copy(k, 0, t).wait_send()
        for j in range(1, chips):
            x_copy(k, j).wait_send()
            gather_copy(k, j, t).wait_send()
            pass_copy(k, j, behind(j) * 2 + core).wait_send()
        return 0

    lax.fori_loop(0, chunks, drain, 0)
    for b in range(tensor):
        for m in range(micro):
            out_copy(b, m).wait()


def per_device(sections, tensor, hidden, down_weight, residual, norm_gain, qkv_weight):
    _, micro, tokens, depth = hidden.shape
    local, features = residual.shape[2:]
    columns = qkv_weight.shape[2]
    chips = tensor // 2
    chunks = CHUNKS
    width = features // chunks
    dma = pltpu.SemaphoreType.DMA
    anywhere = pl.BlockSpec(memory_space=pl.ANY)
    return pl.pallas_call(
        functools.partial(kernel, sections, tensor),
        out_shape=(
            jax.ShapeDtypeStruct((1, micro, local, features), BF16),
            jax.ShapeDtypeStruct((1, micro, tokens, columns), BF16),
        ),
        in_specs=[anywhere, anywhere, anywhere, pl.BlockSpec(memory_space=pltpu.VMEM), anywhere],
        out_specs=(anywhere, anywhere),
        scratch_shapes=[
            pltpu.VMEM((2, chips, micro, local, depth), BF16),
            pltpu.VMEM((SLABS, depth, width), BF16),
            pltpu.VMEM((chunks, width, columns), BF16),
            pltpu.VMEM((micro, local, features), BF16),
            pltpu.VMEM((2, chips, micro, local, width), F32),
            pltpu.VMEM((chunks, chips, micro, local, width), BF16),
            pltpu.VMEM((chunks, chips, micro, local, width), BF16),
            pltpu.VMEM((chunks, chips - 1, micro, local, width), BF16),
            pltpu.VMEM((chunks, chips - 1, micro, local, width), BF16),
            pltpu.VMEM((chunks, micro, local, width), F32),
            pltpu.VMEM((chunks, micro, local, width), BF16),
            pltpu.VMEM((chunks, tensor, micro, local, width), BF16),
            pltpu.VMEM((micro * tokens, columns), F32),
            pltpu.VMEM((micro * tokens, 128), F32),
            pltpu.VMEM((tensor, micro, local, columns), BF16),
            dma((2, chips, micro)), dma((SLABS,)), dma((chunks,)), dma, dma((chunks,)), dma((tensor, micro)),
            dma((chunks,)), dma((chunks,)),
            dma((chunks, chips - 1)), dma((chunks, chips - 1)),
            dma((chunks,)), dma((chunks,)),
            dma((chunks, chips - 1)), dma((chunks, chips - 1)),
            dma((chunks, chips)), dma((chunks, chips)),
        ],
        compiler_params=pltpu.CompilerParams(
            collective_id=0, has_side_effects=True, vmem_limit_bytes=60 * 1024 * 1024
        ),
    )(hidden, down_weight, residual, norm_gain, qkv_weight)


def solution(mesh):
    placed = (
        P("section", "dp", None, "tensor"),
        P("section", "tensor", None),
        P("section", "dp", "tensor", None),
        P("section", None),
        P("section", None, "tensor"),
    )
    return jax.shard_map(
        functools.partial(per_device, mesh.shape["section"], mesh.shape["tensor"]),
        mesh=mesh,
        in_specs=placed,
        out_specs=(P("section", "dp", "tensor", None), P("section", "dp", None, "tensor")),
        check_vma=False,
    )
```

```python
import functools

import jax
import jax.numpy as jnp
from jax import lax
from jax.experimental import pallas as pl
from jax.experimental.pallas import tpu as pltpu
from jax.sharding import PartitionSpec as P

MESH = pl.DeviceIdType.MESH
F32 = jnp.float32
BF16 = jnp.bfloat16
CHUNKS = 8
SLABS = 3
LAG_SUM, LAG_HAND, LAG_PASS, LAG_PROJ = 2, 4, 5, 6


def kernel(
    sections, tensor, hidden, weight, residual, gain_in, projector,
    carried_out, projected_out,
    rows, slab, qkv, res, gain, own, core_send, core_recv, x_send, x_recv, base, stream, carried, acc, squares, out,
    hidden_sem, slab_sem, qkv_sem, res_sem, gain_sem, carried_sem, out_sem,
    core_ss, core_rs, x_ss, x_rs, y_ss, y_rs, g_ss, g_rs, c_ss, c_rs,
):
    chips = tensor // 2
    chunks, micro, local, width = stream.shape
    features = chunks * width
    depth = rows.shape[-1]
    half = chips * micro * local
    s = lax.axis_index("section")
    t = lax.axis_index("tensor")
    chip, core = t // 2, lax.rem(t, 2)
    sibling = chip * 2 + 1 - core
    following = lax.rem(s + 1, sections)
    previous = lax.rem(s + sections - 1, sections)

    def ahead(j):
        return lax.rem(chip + j, chips)

    def behind(j):
        return lax.rem(chip + chips - j, chips)

    def hidden_copy(side, c, m):
        lane = 1 - core if side == 0 else core
        first = pl.multiple_of((c * 2 + lane) * local, local)
        return pltpu.make_async_copy(
            hidden.at[0, m, pl.ds(first, local), :], rows.at[side, c, m], hidden_sem.at[side, c, m]
        )

    def columns(k):
        return pl.ds(pl.multiple_of(k * width, width), width)

    def slab_copy(k):
        slot = lax.rem(k, SLABS)
        return pltpu.make_async_copy(weight.at[0, :, columns(k)], slab.at[slot], slab_sem.at[slot])

    def qkv_copy(k):
        return pltpu.make_async_copy(projector.at[0, columns(k), :], qkv.at[k], qkv_sem.at[k])

    res_copy = pltpu.make_async_copy(residual.at[0], res, res_sem)
    gain_copy = pltpu.make_async_copy(gain_in, gain, gain_sem)

    def carried_copy(k):
        return pltpu.make_async_copy(carried.at[k, core, chip], carried_out.at[0, :, :, columns(k)], carried_sem.at[k])

    def out_copy(side, c, m):
        lane = core if side == 0 else 1 - core
        first = pl.multiple_of((c * 2 + lane) * local, local)
        return pltpu.make_async_copy(
            out.at[side, c, m], projected_out.at[0, m, pl.ds(first, local), :], out_sem.at[side, c, m]
        )

    def core_copy(k):
        return pltpu.make_async_remote_copy(
            src_ref=core_send.at[k], dst_ref=core_recv.at[k], send_sem=core_ss.at[k], recv_sem=core_rs.at[k],
            device_id={"tensor": sibling}, device_id_type=MESH,
        )

    def x_copy(k, j):
        return pltpu.make_async_remote_copy(
            src_ref=x_send.at[k, j - 1], dst_ref=x_recv.at[k, j - 1],
            send_sem=x_ss.at[k, j - 1], recv_sem=x_rs.at[k, j - 1],
            device_id={"tensor": ahead(j) * 2 + core}, device_id_type=MESH,
        )

    def y_copy(k):
        return pltpu.make_async_remote_copy(
            src_ref=stream.at[k], dst_ref=carried.at[k, core, chip], send_sem=y_ss.at[k], recv_sem=y_rs.at[k],
            device_id={"section": following}, device_id_type=MESH,
        )

    def gather_copy(k, j, block):
        block = (core, block)
        return pltpu.make_async_remote_copy(
            src_ref=carried.at[k, *block], dst_ref=carried.at[k, *block],
            send_sem=g_ss.at[k, j - 1], recv_sem=g_rs.at[k, j - 1],
            device_id={"tensor": ahead(j) * 2 + core}, device_id_type=MESH,
        )

    def pass_copy(k, j, lane, block):
        block = (lane, block)
        return pltpu.make_async_remote_copy(
            src_ref=carried.at[k, *block], dst_ref=carried.at[k, *block],
            send_sem=c_ss.at[k, j], recv_sem=c_rs.at[k, j],
            device_id={"tensor": sibling}, device_id_type=MESH,
        )

    def hidden_start(side):
        for c in range(chips):
            for m in range(micro):
                hidden_copy(side, c, m).start()

    def hidden_wait(side):
        for c in range(chips):
            for m in range(micro):
                hidden_copy(side, c, m).wait()

    hidden_start(0)
    slab_copy(0).start()

    barrier = pltpu.get_barrier_semaphore()
    pl.semaphore_signal(barrier, inc=1, device_id={"tensor": sibling}, device_id_type=MESH)
    for j in range(1, chips):
        pl.semaphore_signal(barrier, inc=1, device_id={"tensor": ahead(j) * 2 + core}, device_id_type=MESH)
    pl.semaphore_signal(barrier, inc=1, device_id={"section": following}, device_id_type=MESH)
    if sections > 2:
        pl.semaphore_signal(barrier, inc=1, device_id={"section": previous}, device_id_type=MESH)
    pl.semaphore_wait(barrier, chips + (2 if sections > 2 else 1))

    acc[...] = jnp.zeros_like(acc)
    squares[...] = jnp.zeros_like(squares)

    def multiply(side, slot):
        product = jnp.dot(rows[side].reshape(half, depth), slab[slot], preferred_element_type=F32)
        return product.reshape(chips, micro, local, width)

    def project(k, side):
        lane = core if side == 0 else 1 - core
        values = carried[k, lane].reshape(half, width).astype(F32)
        squared = values * values
        part = squared[:, :128]
        for first in range(128, width, 128):
            part = part + squared[:, first:first + 128]
        squares[side] += part
        scaled = (values * gain[:, columns(k)]).astype(BF16)
        acc[side] += jnp.dot(scaled, qkv[k], preferred_element_type=F32)

    def finish(side):
        mean = jnp.sum(squares[side], axis=-1, keepdims=True) * (1.0 / features)
        value = acc[side] * lax.rsqrt(mean + 1e-05)
        out[side] = value.astype(BF16).reshape(out.shape[1:])
        for c in range(chips):
            for m in range(micro):
                out_copy(side, c, m).start()

    def step(i, _):
        @pl.when(i < chunks)
        def _():
            slot = lax.rem(i, SLABS)

            @pl.when(i == 0)
            def _():
                hidden_wait(0)

            slab_copy(i).wait()

            @pl.when(i == 0)
            def _():
                hidden_start(1)
                res_copy.start()
                gain_copy.start()
                for k in range(1, SLABS):
                    slab_copy(k).start()

            core_send[i] = multiply(0, slot).astype(BF16)
            core_copy(i).start()

            @pl.when(i == 0)
            def _():
                hidden_wait(1)
                res_copy.wait()
                gain_copy.wait()

            own[...] = multiply(1, slot)

            @pl.when(i + SLABS < chunks)
            def _():
                slab_copy(i + SLABS).start()

            qkv_copy(i).start()
            core_copy(i).wait_recv()
            for j in range(1, chips):
                x_send[i, j - 1] = (own[ahead(j)] + core_recv[i, ahead(j)].astype(F32)).astype(BF16)
                x_copy(i, j).start()
            base[i] = own[chip] + core_recv[i, chip].astype(F32) + res[:, :, columns(i)].astype(F32)

        k_sum = i - LAG_SUM

        @pl.when((k_sum >= 0) & (k_sum < chunks))
        def _():
            k = k_sum
            value = base[k]
            for j in range(1, chips):
                x_copy(k, j).wait_recv()
                value = value + x_recv[k, j - 1].astype(F32)
            stream[k] = value.astype(BF16)
            y_copy(k).start()

        k_hand = i - LAG_HAND

        @pl.when((k_hand >= 0) & (k_hand < chunks))
        def _():
            k = k_hand
            y_copy(k).wait_recv()
            for j in range(1, chips):
                gather_copy(k, j, chip).start()
            pass_copy(k, 0, core, chip).start()
            carried_copy(k).start()

        k_proj = i - LAG_PROJ

        @pl.when((k_proj >= 0) & (k_proj < chunks))
        def _():
            k = k_proj
            for j in range(chips):
                pass_copy(k, j, 1 - core, behind(j)).wait_recv()
            project(k, 1)

        k_pass = i - LAG_PASS

        @pl.when((k_pass >= 0) & (k_pass < chunks))
        def _():
            k = k_pass
            for j in range(1, chips):
                gather_copy(k, j, behind(j)).wait_recv()
                pass_copy(k, j, core, behind(j)).start()
            qkv_copy(k).wait()
            project(k, 0)

            @pl.when(k == chunks - 1)
            def _():
                finish(0)

        return 0

    lax.fori_loop(0, chunks + LAG_PROJ, step, 0)
    finish(1)

    def drain(k, _):
        core_copy(k).wait_send()
        y_copy(k).wait_send()
        carried_copy(k).wait()
        pass_copy(k, 0, core, chip).wait_send()
        for j in range(1, chips):
            x_copy(k, j).wait_send()
            gather_copy(k, j, chip).wait_send()
            pass_copy(k, j, core, behind(j)).wait_send()
        return 0

    lax.fori_loop(0, chunks, drain, 0)
    for side in range(2):
        for c in range(chips):
            for m in range(micro):
                out_copy(side, c, m).wait()


def per_device(sections, tensor, hidden, down_weight, residual, norm_gain, qkv_weight):
    _, micro, tokens, depth = hidden.shape
    local, features = residual.shape[2:]
    columns = qkv_weight.shape[2]
    chips = tensor // 2
    chunks = CHUNKS
    width = features // chunks
    dma = pltpu.SemaphoreType.DMA
    anywhere = pl.BlockSpec(memory_space=pl.ANY)
    return pl.pallas_call(
        functools.partial(kernel, sections, tensor),
        out_shape=(
            jax.ShapeDtypeStruct((1, micro, local, features), BF16),
            jax.ShapeDtypeStruct((1, micro, tokens, columns), BF16),
        ),
        in_specs=[pl.BlockSpec(memory_space=pltpu.HBM)] * 5,
        out_specs=(anywhere, anywhere),
        scratch_shapes=[
            pltpu.VMEM((2, chips, micro, local, depth), BF16),
            pltpu.VMEM((SLABS, depth, width), BF16),
            pltpu.VMEM((chunks, width, columns), BF16),
            pltpu.VMEM((micro, local, features), BF16),
            pltpu.VMEM((1, features), F32),
            pltpu.VMEM((chips, micro, local, width), F32),
            pltpu.VMEM((chunks, chips, micro, local, width), BF16),
            pltpu.VMEM((chunks, chips, micro, local, width), BF16),
            pltpu.VMEM((chunks, chips - 1, micro, local, width), BF16),
            pltpu.VMEM((chunks, chips - 1, micro, local, width), BF16),
            pltpu.VMEM((chunks, micro, local, width), F32),
            pltpu.VMEM((chunks, micro, local, width), BF16),
            pltpu.VMEM((chunks, 2, chips, micro, local, width), BF16),
            pltpu.VMEM((2, micro * tokens // 2, columns), F32),
            pltpu.VMEM((2, micro * tokens // 2, 128), F32),
            pltpu.VMEM((2, chips, micro, local, columns), BF16),
            dma((2, chips, micro)), dma((SLABS,)), dma((chunks,)), dma, dma, dma((chunks,)), dma((2, chips, micro)),
            dma((chunks,)), dma((chunks,)),
            dma((chunks, chips - 1)), dma((chunks, chips - 1)),
            dma((chunks,)), dma((chunks,)),
            dma((chunks, chips - 1)), dma((chunks, chips - 1)),
            dma((chunks, chips)), dma((chunks, chips)),
        ],
        compiler_params=pltpu.CompilerParams(
            collective_id=0, has_side_effects=True, vmem_limit_bytes=50 * 1024 * 1024
        ),
    )(hidden, down_weight, residual, norm_gain, qkv_weight)


def solution(mesh):
    placed = (
        P("section", "dp", None, "tensor"),
        P("section", "tensor", None),
        P("section", "dp", "tensor", None),
        P("section", None),
        P("section", None, "tensor"),
    )
    return jax.shard_map(
        functools.partial(per_device, mesh.shape["section"], mesh.shape["tensor"]),
        mesh=mesh,
        in_specs=placed,
        out_specs=(P("section", "dp", "tensor", None), P("section", "dp", None, "tensor")),
        check_vma=False,
    )
```

```python
import functools

import jax
import jax.numpy as jnp
from jax import lax
from jax.experimental import pallas as pl
from jax.experimental.pallas import tpu as pltpu
from jax.sharding import PartitionSpec as P

MESH = pl.DeviceIdType.MESH
F32 = jnp.float32
BF16 = jnp.bfloat16
CHUNKS = 8
SLABS = 3
LAG_SUM, LAG_HAND, LAG_PASS, LAG_PROJ = 2, 4, 5, 6


def kernel(
    sections, tensor, hidden, weight, residual, gain_in, projector,
    carried_out, projected_out,
    rows, slab, qkv, res, gain, own, core_send, core_recv, x_send, x_recv, base, stream, carried, acc, squares, out,
    hidden_sem, slab_sem, qkv_sem, res_sem, gain_sem, carried_sem, out_sem,
    core_ss, core_rs, x_ss, x_rs, y_ss, y_rs, g_ss, g_rs, c_ss, c_rs,
):
    chips = tensor // 2
    chunks, micro, local, width = stream.shape
    features = chunks * width
    depth = rows.shape[-1]
    half = chips * micro * local
    s = lax.axis_index("section")
    t = lax.axis_index("tensor")
    chip, core = t // 2, lax.rem(t, 2)
    sibling = chip * 2 + 1 - core
    following = lax.rem(s + 1, sections)
    previous = lax.rem(s + sections - 1, sections)

    def ahead(j):
        return lax.rem(chip + j, chips)

    def behind(j):
        return lax.rem(chip + chips - j, chips)

    def hidden_copy(side, c, m):
        lane = 1 - core if side == 0 else core
        first = pl.multiple_of((c * 2 + lane) * local, local)
        return pltpu.make_async_copy(
            hidden.at[0, m, pl.ds(first, local), :], rows.at[side, c, m], hidden_sem.at[side, c, m]
        )

    def columns(k):
        return pl.ds(pl.multiple_of(k * width, width), width)

    def slab_copy(k, part):
        slot = lax.rem(k, SLABS)
        lines = pl.ds(part * (depth // 2), depth // 2)
        return pltpu.make_async_copy(
            weight.at[0, lines, columns(k)], slab.at[slot, lines], slab_sem.at[slot, part]
        )

    def slab_start(k):
        for part in range(2):
            slab_copy(k, part).start()

    def qkv_copy(k):
        return pltpu.make_async_copy(projector.at[0, columns(k), :], qkv.at[k], qkv_sem.at[k])

    res_copy = pltpu.make_async_copy(residual.at[0], res, res_sem)
    gain_copy = pltpu.make_async_copy(gain_in, gain, gain_sem)

    def carried_copy(k):
        return pltpu.make_async_copy(carried.at[k, core, chip], carried_out.at[0, :, :, columns(k)], carried_sem.at[k])

    def out_copy(side, c, m):
        lane = core if side == 0 else 1 - core
        first = pl.multiple_of((c * 2 + lane) * local, local)
        return pltpu.make_async_copy(
            out.at[side, c, m], projected_out.at[0, m, pl.ds(first, local), :], out_sem.at[side, c, m]
        )

    def core_copy(k):
        return pltpu.make_async_remote_copy(
            src_ref=core_send.at[k], dst_ref=core_recv.at[k], send_sem=core_ss.at[k], recv_sem=core_rs.at[k],
            device_id={"tensor": sibling}, device_id_type=MESH,
        )

    def x_copy(k, j):
        return pltpu.make_async_remote_copy(
            src_ref=x_send.at[k, j - 1], dst_ref=x_recv.at[k, j - 1],
            send_sem=x_ss.at[k, j - 1], recv_sem=x_rs.at[k, j - 1],
            device_id={"tensor": ahead(j) * 2 + core}, device_id_type=MESH,
        )

    def y_copy(k):
        return pltpu.make_async_remote_copy(
            src_ref=stream.at[k], dst_ref=carried.at[k, core, chip], send_sem=y_ss.at[k], recv_sem=y_rs.at[k],
            device_id={"section": following}, device_id_type=MESH,
        )

    def gather_copy(k, j, block):
        block = (core, block)
        return pltpu.make_async_remote_copy(
            src_ref=carried.at[k, *block], dst_ref=carried.at[k, *block],
            send_sem=g_ss.at[k, j - 1], recv_sem=g_rs.at[k, j - 1],
            device_id={"tensor": ahead(j) * 2 + core}, device_id_type=MESH,
        )

    def pass_copy(k, j, lane, block):
        block = (lane, block)
        return pltpu.make_async_remote_copy(
            src_ref=carried.at[k, *block], dst_ref=carried.at[k, *block],
            send_sem=c_ss.at[k, j], recv_sem=c_rs.at[k, j],
            device_id={"tensor": sibling}, device_id_type=MESH,
        )

    def hidden_start(side):
        for c in range(chips):
            for m in range(micro):
                hidden_copy(side, c, m).start()

    def hidden_wait(side):
        for c in range(chips):
            for m in range(micro):
                hidden_copy(side, c, m).wait()

    hidden_start(0)
    slab_start(0)

    barrier = pltpu.get_barrier_semaphore()
    pl.semaphore_signal(barrier, inc=1, device_id={"tensor": sibling}, device_id_type=MESH)
    for j in range(1, chips):
        pl.semaphore_signal(barrier, inc=1, device_id={"tensor": ahead(j) * 2 + core}, device_id_type=MESH)
    pl.semaphore_signal(barrier, inc=1, device_id={"section": following}, device_id_type=MESH)
    if sections > 2:
        pl.semaphore_signal(barrier, inc=1, device_id={"section": previous}, device_id_type=MESH)
    pl.semaphore_wait(barrier, chips + (2 if sections > 2 else 1))

    acc[...] = jnp.zeros_like(acc)
    squares[...] = jnp.zeros_like(squares)

    def multiply(side, slot, part):
        lines = slice(part * (depth // 2), (part + 1) * (depth // 2))
        product = jnp.dot(
            rows[side, ..., lines].reshape(half, depth // 2), slab[slot, lines], preferred_element_type=F32
        )
        return product.reshape(chips, micro, local, width)

    def project(k, side):
        lane = core if side == 0 else 1 - core
        values = carried[k, lane].reshape(half, width).astype(F32)
        squared = values * values
        part = squared[:, :128]
        for first in range(128, width, 128):
            part = part + squared[:, first:first + 128]
        squares[side] += part
        scaled = (values * gain[:, columns(k)]).astype(BF16)
        acc[side] += jnp.dot(scaled, qkv[k], preferred_element_type=F32)

    def finish(side):
        mean = jnp.sum(squares[side], axis=-1, keepdims=True) * (1.0 / features)
        value = acc[side] * lax.rsqrt(mean + 1e-05)
        out[side] = value.astype(BF16).reshape(out.shape[1:])
        for c in range(chips):
            for m in range(micro):
                out_copy(side, c, m).start()

    def step(i, _):
        @pl.when(i < chunks)
        def _():
            slot = lax.rem(i, SLABS)

            @pl.when(i == 0)
            def _():
                hidden_wait(0)

            slab_copy(i, 0).wait()

            @pl.when(i == 0)
            def _():
                hidden_start(1)
                res_copy.start()
                gain_copy.start()
                for k in range(1, SLABS):
                    slab_start(k)

            own[...] = multiply(0, slot, 0)
            slab_copy(i, 1).wait()
            core_send[i] = (own[...] + multiply(0, slot, 1)).astype(BF16)
            core_copy(i).start()

            @pl.when(i == 0)
            def _():
                hidden_wait(1)
                res_copy.wait()
                gain_copy.wait()

            own[...] = multiply(1, slot, 0) + multiply(1, slot, 1)

            @pl.when(i + SLABS < chunks)
            def _():
                slab_start(i + SLABS)

            qkv_copy(i).start()
            core_copy(i).wait_recv()
            for j in range(1, chips):
                x_send[i, j - 1] = (own[ahead(j)] + core_recv[i, ahead(j)].astype(F32)).astype(BF16)
                x_copy(i, j).start()
            base[i] = own[chip] + core_recv[i, chip].astype(F32) + res[:, :, columns(i)].astype(F32)

        k_sum = i - LAG_SUM

        @pl.when((k_sum >= 0) & (k_sum < chunks))
        def _():
            k = k_sum
            value = base[k]
            for j in range(1, chips):
                x_copy(k, j).wait_recv()
                value = value + x_recv[k, j - 1].astype(F32)
            stream[k] = value.astype(BF16)
            y_copy(k).start()

        k_hand = i - LAG_HAND

        @pl.when((k_hand >= 0) & (k_hand < chunks))
        def _():
            k = k_hand
            y_copy(k).wait_recv()
            for j in range(1, chips):
                gather_copy(k, j, chip).start()
            pass_copy(k, 0, core, chip).start()
            carried_copy(k).start()

        k_proj = i - LAG_PROJ

        @pl.when((k_proj >= 0) & (k_proj < chunks))
        def _():
            k = k_proj
            for j in range(chips):
                pass_copy(k, j, 1 - core, behind(j)).wait_recv()
            project(k, 1)

        k_pass = i - LAG_PASS

        @pl.when((k_pass >= 0) & (k_pass < chunks))
        def _():
            k = k_pass
            for j in range(1, chips):
                gather_copy(k, j, behind(j)).wait_recv()
                pass_copy(k, j, core, behind(j)).start()
            qkv_copy(k).wait()
            project(k, 0)

            @pl.when(k == chunks - 1)
            def _():
                finish(0)

        return 0

    lax.fori_loop(0, chunks + LAG_PROJ, step, 0)
    finish(1)

    def drain(k, _):
        core_copy(k).wait_send()
        y_copy(k).wait_send()
        carried_copy(k).wait()
        pass_copy(k, 0, core, chip).wait_send()
        for j in range(1, chips):
            x_copy(k, j).wait_send()
            gather_copy(k, j, chip).wait_send()
            pass_copy(k, j, core, behind(j)).wait_send()
        return 0

    lax.fori_loop(0, chunks, drain, 0)
    for side in range(2):
        for c in range(chips):
            for m in range(micro):
                out_copy(side, c, m).wait()


def per_device(sections, tensor, hidden, down_weight, residual, norm_gain, qkv_weight):
    _, micro, tokens, depth = hidden.shape
    local, features = residual.shape[2:]
    columns = qkv_weight.shape[2]
    chips = tensor // 2
    chunks = CHUNKS
    width = features // chunks
    dma = pltpu.SemaphoreType.DMA
    anywhere = pl.BlockSpec(memory_space=pl.ANY)
    return pl.pallas_call(
        functools.partial(kernel, sections, tensor),
        out_shape=(
            jax.ShapeDtypeStruct((1, micro, local, features), BF16),
            jax.ShapeDtypeStruct((1, micro, tokens, columns), BF16),
        ),
        in_specs=[pl.BlockSpec(memory_space=pltpu.HBM)] * 5,
        out_specs=(anywhere, anywhere),
        scratch_shapes=[
            pltpu.VMEM((2, chips, micro, local, depth), BF16),
            pltpu.VMEM((SLABS, depth, width), BF16),
            pltpu.VMEM((chunks, width, columns), BF16),
            pltpu.VMEM((micro, local, features), BF16),
            pltpu.VMEM((1, features), F32),
            pltpu.VMEM((chips, micro, local, width), F32),
            pltpu.VMEM((chunks, chips, micro, local, width), BF16),
            pltpu.VMEM((chunks, chips, micro, local, width), BF16),
            pltpu.VMEM((chunks, chips - 1, micro, local, width), BF16),
            pltpu.VMEM((chunks, chips - 1, micro, local, width), BF16),
            pltpu.VMEM((chunks, micro, local, width), F32),
            pltpu.VMEM((chunks, micro, local, width), BF16),
            pltpu.VMEM((chunks, 2, chips, micro, local, width), BF16),
            pltpu.VMEM((2, micro * tokens // 2, columns), F32),
            pltpu.VMEM((2, micro * tokens // 2, 128), F32),
            pltpu.VMEM((2, chips, micro, local, columns), BF16),
            dma((2, chips, micro)), dma((SLABS, 2)), dma((chunks,)), dma, dma, dma((chunks,)), dma((2, chips, micro)),
            dma((chunks,)), dma((chunks,)),
            dma((chunks, chips - 1)), dma((chunks, chips - 1)),
            dma((chunks,)), dma((chunks,)),
            dma((chunks, chips - 1)), dma((chunks, chips - 1)),
            dma((chunks, chips)), dma((chunks, chips)),
        ],
        compiler_params=pltpu.CompilerParams(
            collective_id=0, has_side_effects=True, vmem_limit_bytes=50 * 1024 * 1024
        ),
    )(hidden, down_weight, residual, norm_gain, qkv_weight)


def solution(mesh):
    placed = (
        P("section", "dp", None, "tensor"),
        P("section", "tensor", None),
        P("section", "dp", "tensor", None),
        P("section", None),
        P("section", None, "tensor"),
    )
    return jax.shard_map(
        functools.partial(per_device, mesh.shape["section"], mesh.shape["tensor"]),
        mesh=mesh,
        in_specs=placed,
        out_specs=(P("section", "dp", "tensor", None), P("section", "dp", None, "tensor")),
        check_vma=False,
    )
```
